32 devices in a mesh: row: 4 (over y, core), col: 8 (over z, x).
Axes of the slice: x: 2, y: 2, z: 4, core: 2. Of those that a mesh axis runs over, the one named last changes fastest.
Arguments:
- precip: float32 [1024, 4096], P('row', 'col'), may hold values from 0.002 to 0.02
- head: float32 [1024, 4096], P('row', 'col'), may hold values from -4 to 4
- trans_coef: float32 [1024, 4096], P('row', 'col'), may hold values from 0.05 to 0.5
- land: int32 [1024, 4096], P('row', 'col'), may hold values 0 or 1
- dest: int32 [1024, 32], P('row', 'col'), may hold values from 0 to 32767, as said below
- moisture: float32 [32768, 16, 128], P(('row', 'col')), may hold values from 0.08 to 0.42
- ksat: float32 [32768, 128], P(('row', 'col')), may hold values from 0.002 to 0.01
Outputs:
- saturation: float32 [32768, 16, 128], P(('row', 'col'))
- head_new: float32 [1024, 4096], P('row', 'col')
The draws below stay inside these ranges and needn't reach their ends.
Inputs may be any that keep to these rules, and one draw needn't show every extreme that they name: dest is a permutation of 0 .. 32767; its value is an owner's index along row+col times 1024 plus a slot. At most 64 blocks of one device's tile go to one owner, and every device sends exactly 64 to some owner; every owner receives 1024 blocks.
All inputs are finite; a program needn't handle non-finite values. No bound on the sum of `land` on one device may be relied on, other than what follows from the above.
Results may differ from the reference program's by a relative error of at most 0.00002.
Values sent between devices are 32-bit elements; how exact they have to be, the bound alone decides.
A program may use at most 192 MiB of HBM per device.

```python
import math
import jax
import jax.numpy as jnp

L = 16
TR = 256
TC = 512
SWEEPS = 4
SLOTS = 1024
CAP = 64
NR = 1024
NC = 4096
NBLK = 32768
N_ROW = 4
N_COL = 8


def permuted_slot_list(subkey):
    return jax.random.permutation(subkey, SLOTS)


def draw_dest(key, part):
    processor_units = N_ROW * N_COL
    tickets_total = processor_units * CAP
    key_shuffle, key_leading, key_local, slot_key_random = jax.random.split(key, 4)
    tickets = jnp.arange(tickets_total, dtype=jnp.int32) // CAP
    shuffled = jax.random.permutation(key_shuffle, tickets)
    leading = jax.random.randint(key_leading, (), 0, processor_units, dtype=jnp.int32)
    scores = (shuffled != leading).astype(jnp.int32) * tickets_total + jnp.arange(tickets_total, dtype=jnp.int32)
    ranking = jnp.argsort(scores)
    shifts = shuffled[ranking[:SLOTS]]
    worker_rank_here = jax.vmap(permuted_slot_list)(jax.random.split(key_local, processor_units))
    relabel_blocks = jax.vmap(permuted_slot_list)(jax.random.split(slot_key_random, processor_units))
    sources = jnp.arange(processor_units, dtype=jnp.int32)[:, None]
    block_owner_list = (sources + shifts[worker_rank_here]) % processor_units
    slot_number = relabel_blocks[block_owner_list, worker_rank_here]
    target = block_owner_list * SLOTS + slot_number
    layout = target.reshape(N_ROW, N_COL, TR, TC // 128).transpose(0, 2, 1, 3)
    return layout.reshape(NR, NC // 128).astype(jnp.int32)


def place_ends(result, own_key, least, largest):
    shape = result.shape
    spot = [jax.random.randint(jax.random.fold_in(own_key, axis), (), 0, shape[axis]) for axis in range(len(shape))]
    result = result.at[tuple(spot)].set(least)
    longest = shape.index(max(shape))
    spot[longest] = (spot[longest] + 1) % shape[longest]
    return result.at[tuple(spot)].set(largest)


def block_scale(key, extent, shards, least, high):
    gain, own = 1.0, jax.random.fold_in(key, 6)
    for position, parts in shards:
        heights = jnp.exp(jax.random.uniform(jax.random.fold_in(own, position), (parts,), jnp.float32, least / len(shards), high / len(shards)))
        gain = gain * jnp.repeat(heights, extent[position] // parts).reshape([-1 if axis == position else 1 for axis in range(len(extent))])
    return gain


def gaussian(key, dims, deviation, most, cuts=(), kind=jnp.bfloat16):
    gain = block_scale(key, dims, cuts, -0.22, 0.18) if cuts else 1.0
    entries = jax.random.normal(key, dims, jnp.float32) * deviation * gain
    return jnp.minimum(jnp.maximum(entries, -most), most).astype(kind)


def setup_inputs(seed: int = 0) -> dict:
    key_of = jax.random.split(jax.random.key(seed), 8)
    precip = jnp.clip(jnp.exp(math.log(0.02) - 2.30258502 * jax.random.uniform(key_of[0], (NR, NC), jnp.float32) ** block_scale(key_of[0], (NR, NC), ((0, 4), (1, 8)), -0.2, 0.2)), 0.002, 0.02)
    head = gaussian(key_of[1], (NR, NC), 1.0, 4.0, ((0, 4), (1, 8)), jnp.float32)
    trans_coef = jnp.clip(jnp.exp(math.log(0.5) - 2.3025851 * jax.random.uniform(key_of[2], (NR, NC), jnp.float32) ** block_scale(key_of[2], (NR, NC), ((0, 4), (1, 8)), -0.2, 0.2)), 0.05, 0.5)
    land = place_ends((jax.random.randint(key_of[3], (NR, NC), 0, 4) < 3).astype(jnp.int32), jax.random.fold_in(key_of[3], 1), 0, 1)
    dest = draw_dest(jax.random.fold_in(key_of[7], 71), 0)
    moisture = jnp.clip(0.08 + 0.3399999886751175 * jax.random.uniform(key_of[5], (NBLK, L, 128), jnp.float32) ** block_scale(key_of[5], (NBLK, L, 128), ((0, 32),), -0.2, 0.2), 0.08, 0.42)
    ksat = jnp.clip(jnp.exp(math.log(0.01) - 1.6094378 * jax.random.uniform(key_of[6], (NBLK, 128), jnp.float32) ** block_scale(key_of[6], (NBLK, 128), ((0, 32),), -0.2, 0.2)), 0.002, 0.01)
    return {"precip": precip, "head": head, "trans_coef": trans_coef, "land": land, "dest": dest, "moisture": moisture, "ksat": ksat}


layer_depth = 0.1
step_ratio = 0.1
residual_water = 0.05
pore_range = 0.4
diff_length = 0.5
couple_rate = 0.05
recharge_gain = 20.0
store_rate = 0.2


def factor(moisture, ksat):
    layers = moisture.shape[1]
    depths = (jnp.arange(layers, dtype=jnp.float32) + 0.5) * layer_depth
    scaled_k = ksat[:, None, :] * jnp.exp(-depths)[None, :, None]
    wetness = (moisture - residual_water) / pore_range
    conduct = scaled_k * wetness * wetness * wetness
    slopes = 3.0 * scaled_k * wetness * wetness / pore_range
    diffusion = scaled_k * diff_length * (0.2 + wetness * wetness)
    coupling = (diffusion[:, :-1] + diffusion[:, 1:]) / (2.0 * layer_depth)
    subs, pivots, ratios = [], [], []
    for k in range(layers):
        diagonal = step_ratio + jnp.zeros_like(moisture[:, k])
        if k > 0:
            diagonal = diagonal + coupling[:, k - 1]
        if k < layers - 1:
            diagonal = diagonal + coupling[:, k]
        if k == 0:
            diagonal = diagonal + 0.5 * slopes[:, 0]
        if k == layers - 1:
            diagonal = diagonal + 0.5 * slopes[:, k] + couple_rate
        if k > 0:
            sub_term = -(0.5 * slopes[:, k - 1] + coupling[:, k - 1])
            pivot_k = diagonal - sub_term * ratios[k - 1]
        else:
            sub_term = jnp.zeros_like(diagonal)
            pivot_k = diagonal
        if k < layers - 1:
            ratio_k = (0.5 * slopes[:, k + 1] - coupling[:, k]) / pivot_k
        else:
            ratio_k = jnp.zeros_like(diagonal)
        subs.append(sub_term)
        pivots.append(pivot_k)
        ratios.append(ratio_k)
    return conduct, slopes, coupling, subs, pivots, ratios


def solve(moisture, factors, infiltration, owned_head):
    conduct, slopes, coupling, subs, pivots, ratios = factors
    layers = moisture.shape[1]
    face_flux = 0.5 * (conduct[:, :-1] + conduct[:, 1:]) - coupling * (moisture[:, 1:] - moisture[:, :-1])
    table = residual_water + pore_range * jax.nn.sigmoid(owned_head)
    bottom = conduct[:, -1] + couple_rate * (moisture[:, -1] - table)
    reduced = []
    for k in range(layers):
        above = infiltration if k == 0 else face_flux[:, k - 1]
        below = bottom if k == layers - 1 else face_flux[:, k]
        right_side = above - below
        if k > 0:
            right_side = right_side - subs[k] * reduced[k - 1]
        reduced.append(right_side / pivots[k])
    change = [None] * layers
    change[layers - 1] = reduced[layers - 1]
    for k in range(layers - 2, -1, -1):
        change[k] = reduced[k] - ratios[k] * change[k + 1]
    updated = moisture + jnp.stack(change, axis=1)
    saturation = (updated - residual_water) / pore_range
    recharge = bottom + (slopes[:, -1] + couple_rate) * change[layers - 1]
    return saturation, recharge


def relax(source_term, trans_pad, head_pad, land_share):
    center_t = trans_pad[1:-1, 1:-1]
    face_up = 0.5 * (center_t + trans_pad[:-2, 1:-1])
    face_down = 0.5 * (center_t + trans_pad[2:, 1:-1])
    face_left = 0.5 * (center_t + trans_pad[1:-1, :-2])
    face_right = 0.5 * (center_t + trans_pad[1:-1, 2:])
    total_t = face_up + face_down + face_left + face_right
    inflow = face_up * head_pad[:-2, 1:-1] + face_down * head_pad[2:, 1:-1]
    inflow = inflow + face_left * head_pad[1:-1, :-2] + face_right * head_pad[1:-1, 2:]
    return (source_term + inflow) / (store_rate + total_t) * land_share


def reference(precip, head, trans_coef, land, dest, moisture, ksat):
    grid_rows, grid_cols = precip.shape
    count = grid_rows * grid_cols // 128
    land_share = land.astype(jnp.float32)
    infiltration = (precip * land_share).reshape(count, 128)
    head_blocks = head.reshape(count, 128)
    target = dest.reshape(count)
    owned_infil = jnp.zeros_like(infiltration).at[target].set(infiltration)
    owned_head = jnp.zeros_like(head_blocks).at[target].set(head_blocks)
    factors = factor(moisture, ksat)
    saturation, recharge = solve(moisture, factors, owned_infil, owned_head)
    tile_recharge = recharge[target].reshape(grid_rows, grid_cols)
    initial = head * land_share
    transmit = trans_coef * (1.0 + 0.5 * jnp.tanh(head))
    source_term = store_rate * initial + recharge_gain * tile_recharge
    trans_pad = jnp.pad(transmit, 1)
    surface = initial
    for sweep_k in range(SWEEPS):
        surface = relax(source_term, trans_pad, jnp.pad(surface, 1), land_share)
    return saturation, surface
```

```python
import functools
import math

import jax
import jax.numpy as jnp
from jax import lax
from jax.experimental import pallas as pl
from jax.experimental.pallas import tpu as pltpu
from jax.sharding import PartitionSpec as P

SWEEPS = 4
LANES = 128

layer_depth = 0.1
step_ratio = 0.1
residual_water = 0.05
pore_range = 0.4
diff_length = 0.5
couple_rate = 0.05
recharge_gain = 20.0
store_rate = 0.2

VM = pl.BlockSpec(memory_space=pltpu.VMEM)
SM = pl.BlockSpec(memory_space=pltpu.SMEM)


def f32(*shape):
    return jax.ShapeDtypeStruct(shape, jnp.float32)


def pack_kernel(peers, per_peer, src, labels, precip, head, land, out, infil, heads):
    rows, cols = precip.shape
    for j in range(cols // LANES):
        part = pl.ds(j * LANES, LANES)
        infil[pl.ds(j * rows, rows), :] = precip[:, part] * land[:, part].astype(jnp.float32)
        heads[pl.ds(j * rows, rows), :] = head[:, part]

    def body(p, _):
        for r in range(per_peer):
            block = src[p * per_peer + r]
            out[p, pl.ds(r, 1), :] = infil[pl.ds(block, 1), :]
            out[p, pl.ds(per_peer + r, 1), :] = heads[pl.ds(block, 1), :]
        out[p, pl.ds(2 * per_peer, 8), :] = jnp.broadcast_to(labels[pl.ds(p, 1), :], (8, LANES))
        return 0

    lax.fori_loop(0, peers, body, 0)


def owner_kernel(
    peers, per_peer, slots, arrived, rec0, rec_x, rec_y, answer, infil, sig, own_i, own_h, rec
):
    owned = rec0.shape[0]

    def scatter(p, _):
        for r in range(per_peer):
            slot = slots[p * per_peer + r]
            own_i[pl.ds(slot, 1), :] = arrived[p, pl.ds(r, 1), :]
            own_h[pl.ds(slot, 1), :] = arrived[p, pl.ds(per_peer + r, 1), :]
        return 0

    lax.fori_loop(0, peers, scatter, 0)
    rec[pl.ds(owned, 8), :] = jnp.zeros((8, LANES), jnp.float32)

    def combine(g, _):
        part = pl.ds(g * 64, 64)
        inf = own_i[part, :]
        sg = jax.nn.sigmoid(own_h[part, :])
        infil[part, :] = inf
        sig[part, :] = sg
        rec[part, :] = rec0[part, :] + inf * rec_x[part, :] + sg * rec_y[part, :]
        return 0

    lax.fori_loop(0, owned // 64, combine, 0)

    def gather(p, _):
        for r in range(per_peer):
            slot = slots[p * per_peer + r]
            answer[p, pl.ds(r, 1), :] = rec[pl.ds(slot, 1), :]
        return 0

    lax.fori_loop(0, peers, gather, 0)


def factor_kernel(layers, group, moist, ksat, s0, sx, sy, rec0, rec_x, rec_y):
    count = ksat.shape[0]

    def body(step, _):
        base_row = step * group
        rows = pl.ds(pl.multiple_of(base_row, group), group)
        ks = ksat[rows, :]
        ratios, reds, xs = [], [], []
        before = None
        for k in range(layers):
            m = moist[pl.ds(base_row * layers + k, group, stride=layers), :]
            w = (m - residual_water) * (1.0 / pore_range)
            s = ks * math.exp(-(k + 0.5) * layer_depth)
            sw2 = s * (w * w)
            hs = sw2 * (1.5 / pore_range)
            d = s * (0.2 * diff_length / (2.0 * layer_depth)) + sw2 * (
                diff_length / (2.0 * layer_depth)
            )
            hc = 0.5 * (sw2 * w)
            cur = (m, hs, d, hc)
            if before is None:
                before = cur
                g_up = q_up = nsub = None
                continue
            m0, hs0, d0, hc0 = before
            g = d0 + d
            q = (hc0 + hc) - g * (m - m0)
            if g_up is None:
                pivot = step_ratio + g + hs0
                inv = 1.0 / pivot
                reds.append(-q * inv)
                xs.append(inv)
            else:
                pivot = step_ratio + g_up + g - nsub * ratios[-1]
                inv = 1.0 / pivot
                reds.append(((q_up - q) + nsub * reds[-1]) * inv)
                xs.append(nsub * inv * xs[-1])
            ratios.append((g - hs) * inv)
            nsub = hs0 + g
            g_up, q_up = g, q
            before = cur
        m, hs, d, hc = before
        bottom = 2.0 * hc + couple_rate * (m - residual_water)
        pivot = step_ratio + g_up + hs + couple_rate - nsub * ratios[-1]
        inv = 1.0 / pivot
        change = ((q_up - bottom) + nsub * reds[-1]) * inv
        cx = nsub * inv * xs[-1]
        cy = (couple_rate * pore_range) * inv
        gain = 2.0 * hs + couple_rate
        rec0[rows, :] = bottom + gain * change
        rec_x[rows, :] = gain * cx
        rec_y[rows, :] = gain * cy - couple_rate * pore_range
        unit = 1.0 / pore_range
        for k in range(layers - 1, -1, -1):
            if k < layers - 1:
                change = reds[k] + ratios[k] * change
                cx = xs[k] + ratios[k] * cx
                cy = ratios[k] * cy
            m = moist[pl.ds(base_row * layers + k, group, stride=layers), :]
            s0[k, rows, :] = (m + change - residual_water) * unit
            sx[k, rows, :] = cx * unit
            sy[k, rows, :] = cy * unit
        return 0

    lax.fori_loop(0, count // group, body, 0)


def saturation_kernel(layers, s0, sx, sy, infil, sig, out):
    count = infil.shape[0]
    group = 32

    def body(step, _):
        rows = pl.ds(pl.multiple_of(step * group, group), group)
        inf = infil[rows, :]
        sg = sig[rows, :]
        for k in range(layers):
            out[pl.ds(step * group * layers + k, group, stride=layers), :] = (
                s0[k, rows, :] + inf * sx[k, rows, :] + sg * sy[k, rows, :]
            )
        return 0

    lax.fori_loop(0, count // group, body, 0)


def unpack_kernel(position, returned, head, land, source, sorted_rows):
    rows, cols = head.shape

    def body(g, _):
        for u in range(32):
            place = position[g * 32 + u]
            sorted_rows[pl.ds(g * 32 + u, 1), :] = returned[pl.ds(place, 1), :]
        return 0

    lax.fori_loop(0, sorted_rows.shape[0] // 32, body, 0)
    for j in range(cols // LANES):
        part = slice(j * LANES, (j + 1) * LANES)
        source[:, part] = (
            store_rate * (head[:, part] * land[:, part].astype(jnp.float32))
            + recharge_gain * sorted_rows[j * rows : (j + 1) * rows, :]
        )


def relax_kernel(
    src, src_r, src_c, mid, mid_r, mid_c, out, t_ref, s_ref, fu, fd, fl, fr, a, b
):
    rows, cols = src.shape
    high, wide = t_ref.shape

    def place(dst, centre, edge, side):
        dst[0:rows, 0:cols] = centre
        dst[rows:high, 0:cols] = edge
        dst[:, cols:wide] = side

    place(s_ref, src[...], src_r[...], src_c[...])
    place(t_ref, mid[0], mid_r[0], mid_c[0])
    place(a, mid[1], mid_r[1], mid_c[1])
    place(b, mid[2], mid_r[2], mid_c[2])
    for g in range(wide // LANES):
        part = slice(g * LANES, (g + 1) * LANES)
        left = slice((g - 1) % (wide // LANES) * LANES, (g - 1) % (wide // LANES) * LANES + LANES)
        right = slice((g + 1) % (wide // LANES) * LANES, (g + 1) % (wide // LANES) * LANES + LANES)
        lane = lax.broadcasted_iota(jnp.int32, (high, LANES), 1)
        t = t_ref[:, part]
        up = 0.5 * (t + pltpu.roll(t, 1, 0))
        down = 0.5 * (t + pltpu.roll(t, high - 1, 0))
        tl = jnp.where(lane == 0, pltpu.roll(t_ref[:, left], 1, 1), pltpu.roll(t, 1, 1))
        tr = jnp.where(
            lane == LANES - 1,
            pltpu.roll(t_ref[:, right], LANES - 1, 1),
            pltpu.roll(t, LANES - 1, 1),
        )
        lf = 0.5 * (t + tl)
        rt = 0.5 * (t + tr)
        inv = b[:, part] / (store_rate + (up + down + lf + rt))
        fu[:, part] = up * inv
        fd[:, part] = down * inv
        fl[:, part] = lf * inv
        fr[:, part] = rt * inv
        s_ref[:, part] = s_ref[:, part] * inv
    now, later = a, b
    for sweep in range(SWEEPS):
        last = sweep == SWEEPS - 1
        for g in range(wide // LANES):
            if last and g * LANES >= cols:
                continue
            part = slice(g * LANES, (g + 1) * LANES)
            lo = (g - 1) % (wide // LANES) * LANES
            hi = (g + 1) % (wide // LANES) * LANES
            lane = lax.broadcasted_iota(jnp.int32, (high, LANES), 1)
            x = now[:, part]
            xl = jnp.where(
                lane == 0, pltpu.roll(now[:, lo : lo + LANES], 1, 1), pltpu.roll(x, 1, 1)
            )
            xr = jnp.where(
                lane == LANES - 1,
                pltpu.roll(now[:, hi : hi + LANES], LANES - 1, 1),
                pltpu.roll(x, LANES - 1, 1),
            )
            y = s_ref[:, part] + fu[:, part] * pltpu.roll(x, 1, 0)
            y = y + fd[:, part] * pltpu.roll(x, high - 1, 0)
            y = y + (fl[:, part] * xl + fr[:, part] * xr)
            if last:
                out[:, part] = y[0:rows]
            else:
                later[:, part] = y
        now, later = later, now


def halos(block):
    rows, cols = block.shape[-2:]

    def shift(x, axis, step):
        count = lax.axis_size(axis)
        if step > 0:
            pairs = [(i, i + 1) for i in range(count - 1)]
        else:
            pairs = [(i + 1, i) for i in range(count - 1)]
        return lax.ppermute(x, axis, pairs)

    above = shift(block[..., rows - SWEEPS :, :], "row", 1)
    below = shift(block[..., :SWEEPS, :], "row", -1)
    edge = jnp.concatenate([below, above], axis=-2)
    first = jnp.concatenate([block[..., :SWEEPS], edge[..., :SWEEPS]], axis=-2)
    final = jnp.concatenate([block[..., cols - SWEEPS :], edge[..., cols - SWEEPS :]], axis=-2)
    right = shift(first, "col", -1)
    left = shift(final, "col", 1)
    gap = jnp.zeros(right.shape[:-1] + (LANES - 2 * SWEEPS,), jnp.float32)
    side = jnp.concatenate([right, gap, left], axis=-1)
    return edge, side


def on_device(precip, head, trans_coef, land, dest, moisture, ksat):
    tile_rows, tile_cols = precip.shape
    peers = lax.axis_size("row") * lax.axis_size("col")
    owned, layers, _ = moisture.shape
    blocks = tile_rows * tile_cols // LANES
    per_peer = (2 * blocks + peers - 1) // peers
    places = peers * per_peer

    target = dest.T.reshape(blocks)
    owner = target // owned
    slot = target - owner * owned
    one_hot = owner[:, None] == jnp.arange(peers, dtype=jnp.int32)[None, :]
    order = jnp.arange(blocks, dtype=jnp.int32)
    earlier = (order[None, :] < order[:, None]).astype(jnp.bfloat16)
    counts = jnp.dot(earlier, one_hot.astype(jnp.bfloat16), preferred_element_type=jnp.float32)
    rank = jnp.sum(jnp.where(one_hot, counts, 0.0), axis=1).astype(jnp.int32)
    position = owner * per_peer + rank
    at_rank = rank[:, None] == jnp.arange(per_peer, dtype=jnp.int32)[None, :]
    values = jnp.concatenate(
        [
            jnp.where(at_rank, order.astype(jnp.float32)[:, None], 0.0),
            jnp.where(at_rank, (slot - owned).astype(jnp.float32)[:, None], 0.0),
        ],
        axis=1,
    )
    table = lax.dot_general(
        one_hot.astype(jnp.float32),
        values,
        (((0,), (0,)), ((), ())),
        precision=lax.Precision.HIGHEST,
        preferred_element_type=jnp.float32,
    )
    slot_source = table[:, :per_peer].astype(jnp.int32).reshape(places)
    labels = jnp.pad(table[:, per_peer:] + float(owned), ((0, 0), (0, LANES - per_peer)))

    depth = 2 * per_peer + 8
    outgoing = pl.pallas_call(
        functools.partial(pack_kernel, peers, per_peer),
        out_shape=f32(peers, depth, LANES),
        in_specs=[SM, VM, VM, VM, VM],
        out_specs=VM,
        scratch_shapes=[pltpu.VMEM((blocks, LANES), jnp.float32)] * 2,
    )(slot_source, labels, precip, head, land)
    arrived = lax.all_to_all(outgoing, ("row", "col"), split_axis=0, concat_axis=0, tiled=True)

    land_share = land.astype(jnp.float32)
    transmit = trans_coef * (1.0 + 0.5 * jnp.tanh(head))
    fixed = jnp.stack([transmit, head * land_share, land_share])
    fixed_r, fixed_c = halos(fixed)

    step = 128
    flat = moisture.reshape(owned * layers, LANES)
    layered = pl.BlockSpec((layers, step, LANES), lambda i: (0, i, 0))
    single = pl.BlockSpec((step, LANES), lambda i: (i, 0))
    natural = pl.BlockSpec((step * layers, LANES), lambda i: (i, 0))
    s0, sx, sy, rec0, rec_x, rec_y = pl.pallas_call(
        functools.partial(factor_kernel, layers, 32),
        grid=(owned // step,),
        out_shape=[f32(layers, owned, LANES)] * 3 + [f32(owned, LANES)] * 3,
        in_specs=[natural, single],
        out_specs=[layered] * 3 + [single] * 3,
        cost_estimate=pl.CostEstimate(
            flops=50 * owned * layers * LANES,
            bytes_accessed=16 * owned * layers * LANES,
            transcendentals=owned * layers * LANES,
        ),
    )(flat, ksat)

    slots = arrived[:, 2 * per_peer, :per_peer].astype(jnp.int32).reshape(places)
    answer, infil, sig = pl.pallas_call(
        functools.partial(owner_kernel, peers, per_peer),
        out_shape=[f32(peers, per_peer, LANES), f32(owned, LANES), f32(owned, LANES)],
        in_specs=[SM, VM, VM, VM, VM],
        out_specs=[VM] * 3,
        scratch_shapes=[pltpu.VMEM((owned + 8, LANES), jnp.float32)] * 3,
    )(slots, arrived, rec0, rec_x, rec_y)
    returned = lax.all_to_all(answer, ("row", "col"), split_axis=0, concat_axis=0, tiled=True)

    saturation = pl.pallas_call(
        functools.partial(saturation_kernel, layers),
        grid=(owned // step,),
        out_shape=f32(owned * layers, LANES),
        in_specs=[layered] * 3 + [single] * 2,
        out_specs=natural,
        cost_estimate=pl.CostEstimate(
            flops=4 * owned * layers * LANES,
            bytes_accessed=16 * owned * layers * LANES,
            transcendentals=0,
        ),
    )(s0, sx, sy, infil, sig).reshape(owned, layers, LANES)

    source = pl.pallas_call(
        unpack_kernel,
        out_shape=f32(tile_rows, tile_cols),
        in_specs=[SM, VM, VM, VM],
        out_specs=VM,
        scratch_shapes=[pltpu.VMEM((blocks, LANES), jnp.float32)],
    )(position, returned.reshape(places, LANES), head, land)
    source_r, source_c = halos(source)

    high, wide = tile_rows + 2 * SWEEPS, tile_cols + LANES
    surface = pl.pallas_call(
        relax_kernel,
        out_shape=f32(tile_rows, tile_cols),
        in_specs=[VM] * 6,
        out_specs=VM,
        scratch_shapes=[pltpu.VMEM((high, wide), jnp.float32)] * 8,
    )(source, source_r, source_c, fixed, fixed_r, fixed_c)
    return (saturation, surface)


def solution(mesh):
    tile = P("row", "col")
    placed = (
        tile,
        tile,
        tile,
        tile,
        tile,
        P(("row", "col"), None, None),
        P(("row", "col"), None),
    )
    return jax.shard_map(
        on_device,
        mesh=mesh,
        in_specs=placed,
        out_specs=(P(("row", "col"), None, None), P("row", "col")),
        check_vma=False,
    )
```

```python
import functools
import math

import jax
import jax.numpy as jnp
from jax import lax
from jax.experimental import pallas as pl
from jax.experimental.pallas import tpu as pltpu
from jax.sharding import PartitionSpec as P

SWEEPS = 4
LANES = 128

layer_depth = 0.1
step_ratio = 0.1
residual_water = 0.05
pore_range = 0.4
diff_length = 0.5
couple_rate = 0.05
recharge_gain = 20.0
store_rate = 0.2

VM = pl.BlockSpec(memory_space=pltpu.VMEM)
SM = pl.BlockSpec(memory_space=pltpu.SMEM)


def f32(*shape):
    return jax.ShapeDtypeStruct(shape, jnp.float32)


def pack_kernel(peers, per_peer, src, labels, precip, head, land, out, infil, heads):
    rows, cols = precip.shape
    for j in range(cols // LANES):
        part = pl.ds(j * LANES, LANES)
        infil[pl.ds(j * rows, rows), :] = precip[:, part] * land[:, part].astype(jnp.float32)
        heads[pl.ds(j * rows, rows), :] = head[:, part]

    def body(p, _):
        for r in range(per_peer):
            block = src[p * per_peer + r]
            out[p, pl.ds(r, 1), :] = infil[pl.ds(block, 1), :]
            out[p, pl.ds(per_peer + r, 1), :] = heads[pl.ds(block, 1), :]
        out[p, pl.ds(2 * per_peer, 8), :] = jnp.broadcast_to(labels[pl.ds(p, 1), :], (8, LANES))
        return 0

    lax.fori_loop(0, peers, body, 0)


def owner_kernel(
    peers, per_peer, slots, arrived, rec0, rec_x, rec_y, answer, infil, sig, own_i, own_h, rec
):
    owned = rec0.shape[0]

    def scatter(p, _):
        for r in range(per_peer):
            slot = slots[p * per_peer + r]
            own_i[pl.ds(slot, 1), :] = arrived[p, pl.ds(r, 1), :]
            own_h[pl.ds(slot, 1), :] = arrived[p, pl.ds(per_peer + r, 1), :]
        return 0

    lax.fori_loop(0, peers, scatter, 0)
    rec[pl.ds(owned, 8), :] = jnp.zeros((8, LANES), jnp.float32)

    def combine(g, _):
        part = pl.ds(g * 64, 64)
        inf = own_i[part, :]
        sg = jax.nn.sigmoid(own_h[part, :])
        infil[part, :] = inf
        sig[part, :] = sg
        rec[part, :] = rec0[part, :] + inf * rec_x[part, :] + sg * rec_y[part, :]
        return 0

    lax.fori_loop(0, owned // 64, combine, 0)

    def gather(p, _):
        for r in range(per_peer):
            slot = slots[p * per_peer + r]
            answer[p, pl.ds(r, 1), :] = rec[pl.ds(slot, 1), :]
        return 0

    lax.fori_loop(0, peers, gather, 0)


def factor_kernel(layers, group, moist, ksat, s0, sx, sy, rec0, rec_x, rec_y):
    count = ksat.shape[0]

    def body(step, _):
        base_row = step * group
        rows = pl.ds(pl.multiple_of(base_row, group), group)
        ks = ksat[rows, :]
        ratios, reds, xs = [], [], []
        before = None
        for k in range(layers):
            m = moist[pl.ds(base_row * layers + k, group, stride=layers), :]
            w = (m - residual_water) * (1.0 / pore_range)
            s = ks * math.exp(-(k + 0.5) * layer_depth)
            sw2 = s * (w * w)
            hs = sw2 * (1.5 / pore_range)
            d = s * (0.2 * diff_length / (2.0 * layer_depth)) + sw2 * (
                diff_length / (2.0 * layer_depth)
            )
            hc = 0.5 * (sw2 * w)
            cur = (m, hs, d, hc)
            if before is None:
                before = cur
                g_up = q_up = nsub = None
                continue
            m0, hs0, d0, hc0 = before
            g = d0 + d
            q = (hc0 + hc) - g * (m - m0)
            if g_up is None:
                pivot = step_ratio + g + hs0
                inv = 1.0 / pivot
                reds.append(-q * inv)
                xs.append(inv)
            else:
                pivot = step_ratio + g_up + g - nsub * ratios[-1]
                inv = 1.0 / pivot
                reds.append(((q_up - q) + nsub * reds[-1]) * inv)
                xs.append(nsub * inv * xs[-1])
            ratios.append((g - hs) * inv)
            nsub = hs0 + g
            g_up, q_up = g, q
            before = cur
        m, hs, d, hc = before
        bottom = 2.0 * hc + couple_rate * (m - residual_water)
        pivot = step_ratio + g_up + hs + couple_rate - nsub * ratios[-1]
        inv = 1.0 / pivot
        change = ((q_up - bottom) + nsub * reds[-1]) * inv
        cx = nsub * inv * xs[-1]
        cy = (couple_rate * pore_range) * inv
        gain = 2.0 * hs + couple_rate
        rec0[rows, :] = bottom + gain * change
        rec_x[rows, :] = gain * cx
        rec_y[rows, :] = gain * cy - couple_rate * pore_range
        unit = 1.0 / pore_range
        for k in range(layers - 1, -1, -1):
            if k < layers - 1:
                change = reds[k] + ratios[k] * change
                cx = xs[k] + ratios[k] * cx
                cy = ratios[k] * cy
            m = moist[pl.ds(base_row * layers + k, group, stride=layers), :]
            s0[k, rows, :] = (m + change - residual_water) * unit
            sx[k, rows, :] = cx * unit
            sy[k, rows, :] = cy * unit
        return 0

    lax.fori_loop(0, count // group, body, 0)


def saturation_kernel(layers, s0, sx, sy, infil, sig, out):
    count = infil.shape[0]
    group = 32

    def body(step, _):
        rows = pl.ds(pl.multiple_of(step * group, group), group)
        inf = infil[rows, :]
        sg = sig[rows, :]
        for k in range(layers):
            out[pl.ds(step * group * layers + k, group, stride=layers), :] = (
                s0[k, rows, :] + inf * sx[k, rows, :] + sg * sy[k, rows, :]
            )
        return 0

    lax.fori_loop(0, count // group, body, 0)


def unpack_kernel(position, returned, head, land, source, sorted_rows):
    rows, cols = head.shape

    def body(g, _):
        for u in range(32):
            place = position[g * 32 + u]
            sorted_rows[pl.ds(g * 32 + u, 1), :] = returned[pl.ds(place, 1), :]
        return 0

    lax.fori_loop(0, sorted_rows.shape[0] // 32, body, 0)
    for j in range(cols // LANES):
        part = slice(j * LANES, (j + 1) * LANES)
        source[:, part] = (
            store_rate * (head[:, part] * land[:, part].astype(jnp.float32))
            + recharge_gain * sorted_rows[j * rows : (j + 1) * rows, :]
        )


def relax_kernel(
    src, src_r, src_c, mid, mid_r, mid_c, out, t_ref, s_ref, fu, fd, fl, fr, a, b
):
    rows, cols = src.shape
    high, wide = t_ref.shape

    def place(dst, centre, edge, side):
        dst[0:rows, 0:cols] = centre
        dst[rows:high, 0:cols] = edge
        dst[:, cols:wide] = side

    place(s_ref, src[...], src_r[...], src_c[...])
    place(t_ref, mid[0], mid_r[0], mid_c[0])
    place(a, mid[1], mid_r[1], mid_c[1])
    place(b, mid[2], mid_r[2], mid_c[2])
    for g in range(wide // LANES):
        part = slice(g * LANES, (g + 1) * LANES)
        left = slice((g - 1) % (wide // LANES) * LANES, (g - 1) % (wide // LANES) * LANES + LANES)
        right = slice((g + 1) % (wide // LANES) * LANES, (g + 1) % (wide // LANES) * LANES + LANES)
        lane = lax.broadcasted_iota(jnp.int32, (high, LANES), 1)
        t = t_ref[:, part]
        up = 0.5 * (t + pltpu.roll(t, 1, 0))
        down = 0.5 * (t + pltpu.roll(t, high - 1, 0))
        tl = jnp.where(lane == 0, pltpu.roll(t_ref[:, left], 1, 1), pltpu.roll(t, 1, 1))
        tr = jnp.where(
            lane == LANES - 1,
            pltpu.roll(t_ref[:, right], LANES - 1, 1),
            pltpu.roll(t, LANES - 1, 1),
        )
        lf = 0.5 * (t + tl)
        rt = 0.5 * (t + tr)
        inv = b[:, part] / (store_rate + (up + down + lf + rt))
        fu[:, part] = up * inv
        fd[:, part] = down * inv
        fl[:, part] = lf * inv
        fr[:, part] = rt * inv
        s_ref[:, part] = s_ref[:, part] * inv
    now, later = a, b
    for sweep in range(SWEEPS):
        last = sweep == SWEEPS - 1
        for g in range(wide // LANES):
            if last and g * LANES >= cols:
                continue
            part = slice(g * LANES, (g + 1) * LANES)
            lo = (g - 1) % (wide // LANES) * LANES
            hi = (g + 1) % (wide // LANES) * LANES
            lane = lax.broadcasted_iota(jnp.int32, (high, LANES), 1)
            x = now[:, part]
            xl = jnp.where(
                lane == 0, pltpu.roll(now[:, lo : lo + LANES], 1, 1), pltpu.roll(x, 1, 1)
            )
            xr = jnp.where(
                lane == LANES - 1,
                pltpu.roll(now[:, hi : hi + LANES], LANES - 1, 1),
                pltpu.roll(x, LANES - 1, 1),
            )
            y = s_ref[:, part] + fu[:, part] * pltpu.roll(x, 1, 0)
            y = y + fd[:, part] * pltpu.roll(x, high - 1, 0)
            y = y + (fl[:, part] * xl + fr[:, part] * xr)
            if last:
                out[:, part] = y[0:rows]
            else:
                later[:, part] = y
        now, later = later, now


def halos(block):
    rows, cols = block.shape[-2:]

    def shift(x, axis, step):
        count = lax.axis_size(axis)
        if step > 0:
            pairs = [(i, i + 1) for i in range(count - 1)]
        else:
            pairs = [(i + 1, i) for i in range(count - 1)]
        return lax.ppermute(x, axis, pairs)

    above = shift(block[..., rows - SWEEPS :, :], "row", 1)
    below = shift(block[..., :SWEEPS, :], "row", -1)
    edge = jnp.concatenate([below, above], axis=-2)
    first = jnp.concatenate([block[..., :SWEEPS], edge[..., :SWEEPS]], axis=-2)
    final = jnp.concatenate([block[..., cols - SWEEPS :], edge[..., cols - SWEEPS :]], axis=-2)
    right = shift(first, "col", -1)
    left = shift(final, "col", 1)
    gap = jnp.zeros(right.shape[:-1] + (LANES - 2 * SWEEPS,), jnp.float32)
    side = jnp.concatenate([right, gap, left], axis=-1)
    return edge, side


def on_device(precip, head, trans_coef, land, dest, moisture, ksat):
    tile_rows, tile_cols = precip.shape
    peers = lax.axis_size("row") * lax.axis_size("col")
    owned, layers, _ = moisture.shape
    blocks = tile_rows * tile_cols // LANES
    per_peer = (2 * blocks + peers - 1) // peers
    places = peers * per_peer

    target = dest.T.reshape(blocks)
    owner = target // owned
    slot = target - owner * owned
    one_hot = owner[:, None] == jnp.arange(peers, dtype=jnp.int32)[None, :]
    order = jnp.arange(blocks, dtype=jnp.int32)
    earlier = (order[None, :] < order[:, None]).astype(jnp.bfloat16)
    counts = jnp.dot(earlier, one_hot.astype(jnp.bfloat16), preferred_element_type=jnp.float32)
    rank = jnp.sum(jnp.where(one_hot, counts, 0.0), axis=1).astype(jnp.int32)
    position = owner * per_peer + rank
    at_rank = rank[:, None] == jnp.arange(per_peer, dtype=jnp.int32)[None, :]
    values = jnp.concatenate(
        [
            jnp.where(at_rank, order.astype(jnp.float32)[:, None], 0.0),
            jnp.where(at_rank, (slot - owned).astype(jnp.float32)[:, None], 0.0),
        ],
        axis=1,
    )
    table = lax.dot_general(
        one_hot.astype(jnp.float32),
        values,
        (((0,), (0,)), ((), ())),
        precision=lax.Precision.HIGHEST,
        preferred_element_type=jnp.float32,
    )
    slot_source = table[:, :per_peer].astype(jnp.int32).reshape(places)
    labels = jnp.pad(table[:, per_peer:] + float(owned), ((0, 0), (0, LANES - per_peer)))

    depth = 2 * per_peer + 8
    outgoing = pl.pallas_call(
        functools.partial(pack_kernel, peers, per_peer),
        out_shape=f32(peers, depth, LANES),
        in_specs=[SM, VM, VM, VM, VM],
        out_specs=VM,
        scratch_shapes=[pltpu.VMEM((blocks, LANES), jnp.float32)] * 2,
    )(slot_source, labels, precip, head, land)
    arrived = lax.all_to_all(outgoing, ("row", "col"), split_axis=0, concat_axis=0, tiled=True)

    land_share = land.astype(jnp.float32)
    transmit = trans_coef * (1.0 + 0.5 * jnp.tanh(head))
    fixed = jnp.stack([transmit, head * land_share, land_share])
    fixed_r, fixed_c = halos(fixed)

    step = 128
    flat = moisture.reshape(owned * layers, LANES)
    layered = pl.BlockSpec((layers, step, LANES), lambda i: (0, i, 0))
    single = pl.BlockSpec((step, LANES), lambda i: (i, 0))
    natural = pl.BlockSpec((step * layers, LANES), lambda i: (i, 0))
    s0, sx, sy, rec0, rec_x, rec_y = pl.pallas_call(
        functools.partial(factor_kernel, layers, 32),
        grid=(owned // step,),
        out_shape=[f32(layers, owned, LANES)] * 3 + [f32(owned, LANES)] * 3,
        in_specs=[natural, single],
        out_specs=[layered] * 3 + [single] * 3,
        cost_estimate=pl.CostEstimate(
            flops=50 * owned * layers * LANES,
            bytes_accessed=16 * owned * layers * LANES,
            transcendentals=owned * layers * LANES,
        ),
    )(flat, ksat)

    arrived, fixed_r, fixed_c = lax.optimization_barrier((arrived, fixed_r, fixed_c))
    slots = arrived[:, 2 * per_peer, :per_peer].astype(jnp.int32).reshape(places)
    answer, infil, sig = pl.pallas_call(
        functools.partial(owner_kernel, peers, per_peer),
        out_shape=[f32(peers, per_peer, LANES), f32(owned, LANES), f32(owned, LANES)],
        in_specs=[SM, VM, VM, VM, VM],
        out_specs=[VM] * 3,
        scratch_shapes=[pltpu.VMEM((owned + 8, LANES), jnp.float32)] * 3,
    )(slots, arrived, rec0, rec_x, rec_y)
    returned = lax.all_to_all(answer, ("row", "col"), split_axis=0, concat_axis=0, tiled=True)

    saturation = pl.pallas_call(
        functools.partial(saturation_kernel, layers),
        grid=(owned // step,),
        out_shape=f32(owned * layers, LANES),
        in_specs=[layered] * 3 + [single] * 2,
        out_specs=natural,
        cost_estimate=pl.CostEstimate(
            flops=4 * owned * layers * LANES,
            bytes_accessed=16 * owned * layers * LANES,
            transcendentals=0,
        ),
    )(s0, sx, sy, infil, sig).reshape(owned, layers, LANES)

    source = pl.pallas_call(
        unpack_kernel,
        out_shape=f32(tile_rows, tile_cols),
        in_specs=[SM, VM, VM, VM],
        out_specs=VM,
        scratch_shapes=[pltpu.VMEM((blocks, LANES), jnp.float32)],
    )(position, returned.reshape(places, LANES), head, land)
    source_r, source_c = halos(source)

    high, wide = tile_rows + 2 * SWEEPS, tile_cols + LANES
    surface = pl.pallas_call(
        relax_kernel,
        out_shape=f32(tile_rows, tile_cols),
        in_specs=[VM] * 6,
        out_specs=VM,
        scratch_shapes=[pltpu.VMEM((high, wide), jnp.float32)] * 8,
    )(source, source_r, source_c, fixed, fixed_r, fixed_c)
    return (saturation, surface)


def solution(mesh):
    tile = P("row", "col")
    placed = (
        tile,
        tile,
        tile,
        tile,
        tile,
        P(("row", "col"), None, None),
        P(("row", "col"), None),
    )
    return jax.shard_map(
        on_device,
        mesh=mesh,
        in_specs=placed,
        out_specs=(P(("row", "col"), None, None), P("row", "col")),
        check_vma=False,
    )
```

```python
import functools
import math

import jax
import jax.numpy as jnp
from jax import lax
from jax.experimental import pallas as pl
from jax.experimental.pallas import tpu as pltpu
from jax.sharding import PartitionSpec as P

SWEEPS = 4
LANES = 128

layer_depth = 0.1
step_ratio = 0.1
residual_water = 0.05
pore_range = 0.4
diff_length = 0.5
couple_rate = 0.05
recharge_gain = 20.0
store_rate = 0.2

VM = pl.BlockSpec(memory_space=pltpu.VMEM)
SM = pl.BlockSpec(memory_space=pltpu.SMEM)


def f32(*shape):
    return jax.ShapeDtypeStruct(shape, jnp.float32)


def pack_kernel(peers, per_peer, src, labels, precip, head, land, out, infil, heads):
    rows, cols = precip.shape
    for j in range(cols // LANES):
        part = pl.ds(j * LANES, LANES)
        infil[pl.ds(j * rows, rows), :] = precip[:, part] * land[:, part].astype(jnp.float32)
        heads[pl.ds(j * rows, rows), :] = head[:, part]

    def body(p, _):
        for r in range(per_peer):
            block = src[p * per_peer + r]
            out[p, pl.ds(r, 1), :] = infil[pl.ds(block, 1), :]
            out[p, pl.ds(per_peer + r, 1), :] = heads[pl.ds(block, 1), :]
        out[p, pl.ds(2 * per_peer, 8), :] = jnp.broadcast_to(labels[pl.ds(p, 1), :], (8, LANES))
        return 0

    lax.fori_loop(0, peers, body, 0)


def owner_kernel(
    peers, per_peer, slots, arrived, rec0, rec_x, rec_y, answer, infil, sig, own_i, own_h, rec
):
    owned = rec0.shape[0]

    def scatter(p, _):
        for r in range(per_peer):
            slot = slots[p * per_peer + r]
            own_i[pl.ds(slot, 1), :] = arrived[p, pl.ds(r, 1), :]
            own_h[pl.ds(slot, 1), :] = arrived[p, pl.ds(per_peer + r, 1), :]
        return 0

    lax.fori_loop(0, peers, scatter, 0)
    rec[pl.ds(owned, 8), :] = jnp.zeros((8, LANES), jnp.float32)

    def combine(g, _):
        part = pl.ds(g * 64, 64)
        inf = own_i[part, :]
        sg = jax.nn.sigmoid(own_h[part, :])
        infil[part, :] = inf
        sig[part, :] = sg
        rec[part, :] = rec0[part, :] + inf * rec_x[part, :] + sg * rec_y[part, :]
        return 0

    lax.fori_loop(0, owned // 64, combine, 0)

    def gather(p, _):
        for r in range(per_peer):
            slot = slots[p * per_peer + r]
            answer[p, pl.ds(r, 1), :] = rec[pl.ds(slot, 1), :]
        return 0

    lax.fori_loop(0, peers, gather, 0)


def factor_kernel(layers, group, moist, ksat, s0, sx, sy, rec0, rec_x, rec_y):
    count = ksat.shape[0]

    def body(step, _):
        base_row = step * group
        rows = pl.ds(pl.multiple_of(base_row, group), group)
        ks = ksat[rows, :]
        ratios, reds, xs = [], [], []
        before = None
        for k in range(layers):
            m = moist[pl.ds(base_row * layers + k, group, stride=layers), :]
            w = (m - residual_water) * (1.0 / pore_range)
            s = ks * math.exp(-(k + 0.5) * layer_depth)
            sw2 = s * (w * w)
            hs = sw2 * (1.5 / pore_range)
            d = s * (0.2 * diff_length / (2.0 * layer_depth)) + sw2 * (
                diff_length / (2.0 * layer_depth)
            )
            hc = 0.5 * (sw2 * w)
            cur = (m, hs, d, hc)
            if before is None:
                before = cur
                g_up = q_up = nsub = None
                continue
            m0, hs0, d0, hc0 = before
            g = d0 + d
            q = (hc0 + hc) - g * (m - m0)
            if g_up is None:
                pivot = step_ratio + g + hs0
                inv = 1.0 / pivot
                reds.append(-q * inv)
                xs.append(inv)
            else:
                pivot = step_ratio + g_up + g - nsub * ratios[-1]
                inv = 1.0 / pivot
                reds.append(((q_up - q) + nsub * reds[-1]) * inv)
                xs.append(nsub * inv * xs[-1])
            ratios.append((g - hs) * inv)
            nsub = hs0 + g
            g_up, q_up = g, q
            before = cur
        m, hs, d, hc = before
        bottom = 2.0 * hc + couple_rate * (m - residual_water)
        pivot = step_ratio + g_up + hs + couple_rate - nsub * ratios[-1]
        inv = 1.0 / pivot
        change = ((q_up - bottom) + nsub * reds[-1]) * inv
        cx = nsub * inv * xs[-1]
        cy = (couple_rate * pore_range) * inv
        gain = 2.0 * hs + couple_rate
        rec0[rows, :] = bottom + gain * change
        rec_x[rows, :] = gain * cx
        rec_y[rows, :] = gain * cy - couple_rate * pore_range
        unit = 1.0 / pore_range
        for k in range(layers - 1, -1, -1):
            if k < layers - 1:
                change = reds[k] + ratios[k] * change
                cx = xs[k] + ratios[k] * cx
                cy = ratios[k] * cy
            m = moist[pl.ds(base_row * layers + k, group, stride=layers), :]
            s0[k, rows, :] = (m + change - residual_water) * unit
            sx[k, rows, :] = cx * unit
            sy[k, rows, :] = cy * unit
        return 0

    lax.fori_loop(0, count // group, body, 0)


def saturation_kernel(layers, s0, sx, sy, infil, sig, out):
    count = infil.shape[0]
    group = 32

    def body(step, _):
        rows = pl.ds(pl.multiple_of(step * group, group), group)
        inf = infil[rows, :]
        sg = sig[rows, :]
        for k in range(layers):
            out[pl.ds(step * group * layers + k, group, stride=layers), :] = (
                s0[k, rows, :] + inf * sx[k, rows, :] + sg * sy[k, rows, :]
            )
        return 0

    lax.fori_loop(0, count // group, body, 0)


def unpack_kernel(position, returned, head, land, source, sorted_rows):
    rows, cols = head.shape

    def body(g, _):
        for u in range(32):
            place = position[g * 32 + u]
            sorted_rows[pl.ds(g * 32 + u, 1), :] = returned[pl.ds(place, 1), :]
        return 0

    lax.fori_loop(0, sorted_rows.shape[0] // 32, body, 0)
    for j in range(cols // LANES):
        part = slice(j * LANES, (j + 1) * LANES)
        source[:, part] = (
            store_rate * (head[:, part] * land[:, part].astype(jnp.float32))
            + recharge_gain * sorted_rows[j * rows : (j + 1) * rows, :]
        )


def relax_kernel(
    src, src_r, src_c, mid, mid_r, mid_c, out, t_ref, s_ref, fu, fd, fl, fr, a, b
):
    rows, cols = src.shape
    high, wide = t_ref.shape

    def place(dst, centre, edge, side):
        dst[0:rows, 0:cols] = centre
        dst[rows:high, 0:cols] = edge
        dst[:, cols:wide] = side

    place(s_ref, src[...], src_r[...], src_c[...])
    place(t_ref, mid[0], mid_r[0], mid_c[0])
    place(a, mid[1], mid_r[1], mid_c[1])
    place(b, mid[2], mid_r[2], mid_c[2])
    for g in range(wide // LANES):
        part = slice(g * LANES, (g + 1) * LANES)
        left = slice((g - 1) % (wide // LANES) * LANES, (g - 1) % (wide // LANES) * LANES + LANES)
        right = slice((g + 1) % (wide // LANES) * LANES, (g + 1) % (wide // LANES) * LANES + LANES)
        lane = lax.broadcasted_iota(jnp.int32, (high, LANES), 1)
        t = t_ref[:, part]
        up = 0.5 * (t + pltpu.roll(t, 1, 0))
        down = 0.5 * (t + pltpu.roll(t, high - 1, 0))
        tl = jnp.where(lane == 0, pltpu.roll(t_ref[:, left], 1, 1), pltpu.roll(t, 1, 1))
        tr = jnp.where(
            lane == LANES - 1,
            pltpu.roll(t_ref[:, right], LANES - 1, 1),
            pltpu.roll(t, LANES - 1, 1),
        )
        lf = 0.5 * (t + tl)
        rt = 0.5 * (t + tr)
        inv = b[:, part] / (store_rate + (up + down + lf + rt))
        fu[:, part] = up * inv
        fd[:, part] = down * inv
        fl[:, part] = lf * inv
        fr[:, part] = rt * inv
        s_ref[:, part] = s_ref[:, part] * inv
    now, later = a, b
    for sweep in range(SWEEPS):
        last = sweep == SWEEPS - 1
        for g in range(wide // LANES):
            if last and g * LANES >= cols:
                continue
            part = slice(g * LANES, (g + 1) * LANES)
            lo = (g - 1) % (wide // LANES) * LANES
            hi = (g + 1) % (wide // LANES) * LANES
            lane = lax.broadcasted_iota(jnp.int32, (high, LANES), 1)
            x = now[:, part]
            xl = jnp.where(
                lane == 0, pltpu.roll(now[:, lo : lo + LANES], 1, 1), pltpu.roll(x, 1, 1)
            )
            xr = jnp.where(
                lane == LANES - 1,
                pltpu.roll(now[:, hi : hi + LANES], LANES - 1, 1),
                pltpu.roll(x, LANES - 1, 1),
            )
            y = s_ref[:, part] + fu[:, part] * pltpu.roll(x, 1, 0)
            y = y + fd[:, part] * pltpu.roll(x, high - 1, 0)
            y = y + (fl[:, part] * xl + fr[:, part] * xr)
            if last:
                out[:, part] = y[0:rows]
            else:
                later[:, part] = y
        now, later = later, now


def halos(block):
    rows, cols = block.shape[-2:]

    def shift(x, axis, step):
        count = lax.axis_size(axis)
        if step > 0:
            pairs = [(i, i + 1) for i in range(count - 1)]
        else:
            pairs = [(i + 1, i) for i in range(count - 1)]
        return lax.ppermute(x, axis, pairs)

    above = shift(block[..., rows - SWEEPS :, :], "row", 1)
    below = shift(block[..., :SWEEPS, :], "row", -1)
    edge = jnp.concatenate([below, above], axis=-2)
    first = jnp.concatenate([block[..., :SWEEPS], edge[..., :SWEEPS]], axis=-2)
    final = jnp.concatenate([block[..., cols - SWEEPS :], edge[..., cols - SWEEPS :]], axis=-2)
    right = jnp.swapaxes(shift(jnp.swapaxes(first, -1, -2), "col", -1), -1, -2)
    left = jnp.swapaxes(shift(jnp.swapaxes(final, -1, -2), "col", 1), -1, -2)
    gap = jnp.zeros(right.shape[:-1] + (LANES - 2 * SWEEPS,), jnp.float32)
    side = jnp.concatenate([right, gap, left], axis=-1)
    return edge, side


def on_device(precip, head, trans_coef, land, dest, moisture, ksat):
    tile_rows, tile_cols = precip.shape
    peers = lax.axis_size("row") * lax.axis_size("col")
    owned, layers, _ = moisture.shape
    blocks = tile_rows * tile_cols // LANES
    per_peer = (2 * blocks + peers - 1) // peers
    places = peers * per_peer

    target = dest.T.reshape(blocks)
    owner = target // owned
    slot = target - owner * owned
    one_hot = owner[:, None] == jnp.arange(peers, dtype=jnp.int32)[None, :]
    order = jnp.arange(blocks, dtype=jnp.int32)
    earlier = (order[None, :] < order[:, None]).astype(jnp.bfloat16)
    counts = jnp.dot(earlier, one_hot.astype(jnp.bfloat16), preferred_element_type=jnp.float32)
    rank = jnp.sum(jnp.where(one_hot, counts, 0.0), axis=1).astype(jnp.int32)
    position = owner * per_peer + rank
    at_rank = rank[:, None] == jnp.arange(per_peer, dtype=jnp.int32)[None, :]
    values = jnp.concatenate(
        [
            jnp.where(at_rank, order.astype(jnp.float32)[:, None], 0.0),
            jnp.where(at_rank, (slot - owned).astype(jnp.float32)[:, None], 0.0),
        ],
        axis=1,
    )
    table = lax.dot_general(
        one_hot.astype(jnp.float32),
        values,
        (((0,), (0,)), ((), ())),
        precision=lax.Precision.HIGHEST,
        preferred_element_type=jnp.float32,
    )
    slot_source = table[:, :per_peer].astype(jnp.int32).reshape(places)
    labels = jnp.pad(table[:, per_peer:] + float(owned), ((0, 0), (0, LANES - per_peer)))

    depth = 2 * per_peer + 8
    outgoing = pl.pallas_call(
        functools.partial(pack_kernel, peers, per_peer),
        out_shape=f32(peers, depth, LANES),
        in_specs=[SM, VM, VM, VM, VM],
        out_specs=VM,
        scratch_shapes=[pltpu.VMEM((blocks, LANES), jnp.float32)] * 2,
    )(slot_source, labels, precip, head, land)
    arrived = lax.all_to_all(outgoing, ("row", "col"), split_axis=0, concat_axis=0, tiled=True)

    land_share = land.astype(jnp.float32)
    transmit = trans_coef * (1.0 + 0.5 * jnp.tanh(head))
    fixed = jnp.stack([transmit, head * land_share, land_share])
    fixed_r, fixed_c = halos(fixed)

    step = 128
    flat = moisture.reshape(owned * layers, LANES)
    layered = pl.BlockSpec((layers, step, LANES), lambda i: (0, i, 0))
    single = pl.BlockSpec((step, LANES), lambda i: (i, 0))
    natural = pl.BlockSpec((step * layers, LANES), lambda i: (i, 0))
    s0, sx, sy, rec0, rec_x, rec_y = pl.pallas_call(
        functools.partial(factor_kernel, layers, 32),
        grid=(owned // step,),
        out_shape=[f32(layers, owned, LANES)] * 3 + [f32(owned, LANES)] * 3,
        in_specs=[natural, single],
        out_specs=[layered] * 3 + [single] * 3,
        cost_estimate=pl.CostEstimate(
            flops=50 * owned * layers * LANES,
            bytes_accessed=16 * owned * layers * LANES,
            transcendentals=owned * layers * LANES,
        ),
    )(flat, ksat)

    arrived, fixed_r, fixed_c = lax.optimization_barrier((arrived, fixed_r, fixed_c))
    slots = arrived[:, 2 * per_peer, :per_peer].astype(jnp.int32).reshape(places)
    answer, infil, sig = pl.pallas_call(
        functools.partial(owner_kernel, peers, per_peer),
        out_shape=[f32(peers, per_peer, LANES), f32(owned, LANES), f32(owned, LANES)],
        in_specs=[SM, VM, VM, VM, VM],
        out_specs=[VM] * 3,
        scratch_shapes=[pltpu.VMEM((owned + 8, LANES), jnp.float32)] * 3,
    )(slots, arrived, rec0, rec_x, rec_y)
    returned = lax.all_to_all(answer, ("row", "col"), split_axis=0, concat_axis=0, tiled=True)

    saturation = pl.pallas_call(
        functools.partial(saturation_kernel, layers),
        grid=(owned // step,),
        out_shape=f32(owned * layers, LANES),
        in_specs=[layered] * 3 + [single] * 2,
        out_specs=natural,
        cost_estimate=pl.CostEstimate(
            flops=4 * owned * layers * LANES,
            bytes_accessed=16 * owned * layers * LANES,
            transcendentals=0,
        ),
    )(s0, sx, sy, infil, sig).reshape(owned, layers, LANES)

    source = pl.pallas_call(
        unpack_kernel,
        out_shape=f32(tile_rows, tile_cols),
        in_specs=[SM, VM, VM, VM],
        out_specs=VM,
        scratch_shapes=[pltpu.VMEM((blocks, LANES), jnp.float32)],
    )(position, returned.reshape(places, LANES), head, land)
    source_r, source_c = halos(source)

    high, wide = tile_rows + 2 * SWEEPS, tile_cols + LANES
    surface = pl.pallas_call(
        relax_kernel,
        out_shape=f32(tile_rows, tile_cols),
        in_specs=[VM] * 6,
        out_specs=VM,
        scratch_shapes=[pltpu.VMEM((high, wide), jnp.float32)] * 8,
    )(source, source_r, source_c, fixed, fixed_r, fixed_c)
    return (saturation, surface)


def solution(mesh):
    tile = P("row", "col")
    placed = (
        tile,
        tile,
        tile,
        tile,
        tile,
        P(("row", "col"), None, None),
        P(("row", "col"), None),
    )
    return jax.shard_map(
        on_device,
        mesh=mesh,
        in_specs=placed,
        out_specs=(P(("row", "col"), None, None), P("row", "col")),
        check_vma=False,
    )
```
